32 devices in a mesh: groups: 2 (over y), seq: 8 (over z, x), tensor: 2 (over core).
Axes of the slice: x: 2, y: 2, z: 4, core: 2. Of those that a mesh axis runs over, the one named last changes fastest.
Arguments:
- q_proj: bfloat16 [2048, 8192], P(('groups', 'seq'), 'tensor'), parts along dimension 0, may hold values from -6 to 6
- k_proj: bfloat16 [2048, 8192], P(('groups', 'seq'), 'tensor'), parts along dimension 0, may hold values from -6 to 6
- v_proj: bfloat16 [2048, 8192], P(('groups', 'seq'), 'tensor'), parts along dimension 0, may hold values from -6 to 6
- short_taps: bfloat16 [3, 7, 8192], P(None, None, 'tensor'), may hold values from -2 to 2
- pole_rate: float32 [16, 8192], P(None, 'tensor'), may hold values from 4.8828125e-05 to 0.0333333333
- pole_angle: float32 [16, 8192], P(None, 'tensor'), may hold values from -3.140625 to 3.140625
- residue_re: float32 [16, 8192], P(None, 'tensor'), may hold values from -0.3 to 0.3
- residue_im: float32 [16, 8192], P(None, 'tensor'), may hold values from -0.3 to 0.3
- skip_gain: float32 [8192], P('tensor'), may hold values from -3 to 3
Outputs:
- mixed_out: bfloat16 [2048, 8192], P(('groups', 'seq'), 'tensor'), parts along dimension 0
The draws below stay inside these ranges and needn't reach their ends.
There are 2 independent parts, one for each index of `groups`. The reference program is written for one: setup_inputs(seed, part) draws one part's arguments, and reference() takes and returns one part's arrays. A program takes and returns all parts, laid end to end along the dimension named above; an argument that names none is the same for every part. Nothing has to cross between parts.
All inputs are finite; a program needn't handle non-finite values.
Results may differ from the reference program's by a relative error of at most 0.0049.
Values may be sent and summed in bfloat16 or wider, within the bound.
No kernel may reach another device: no remote copies, remote signals or barrier semaphores. Data moves between devices by JAX's collectives and lax.ppermute only.
A program may use at most 192 MiB of HBM per device.

```python
import math
import jax
import jax.numpy as jnp
from jax import lax

D = 8192
M = 16
SHORT = 7
TOK_DEV = 128
TOKENS = 1024
N_SEQ = 8


def rate_table(key):
    first = jax.random.uniform(jax.random.fold_in(key, 11), (M, D), jnp.float32)
    low = jnp.log(0.05 / TOKENS)
    high = jnp.log(1.0 / 30)
    logs = low + first * (high - low)
    return jnp.exp(logs)


def residue_part(key, salt):
    rates = rate_table(jax.random.fold_in(key, 1))
    base = jnp.clip(jax.random.normal(jax.random.fold_in(key, salt), (M, D), jnp.float32), -4.0, 4.0)
    return base * jnp.sqrt(2.0 * rates) / 4.0


def draw_pole_rate(key, part):
    return rate_table(jax.random.fold_in(key, 1))


def draw_residue_re(key, part):
    return residue_part(key, 2)


def draw_residue_im(key, part):
    return residue_part(key, 3)


def steps_of(rng, shape, split, least, top_value):
    factor_of, own = 1.0, jax.random.fold_in(rng, 6)
    for axis_at, blocks in split:
        steps = jnp.exp(jax.random.uniform(jax.random.fold_in(own, axis_at), (blocks,), jnp.float32, least / len(split), top_value / len(split)))
        factor_of = factor_of * jnp.repeat(steps, shape[axis_at] // blocks).reshape([-1 if axis == axis_at else 1 for axis in range(len(shape))])
    return factor_of


def centred(stream_key, extent, scale, bound, cuts=(), kind=jnp.bfloat16):
    values = scale * jax.random.normal(stream_key, extent, jnp.float32)
    if cuts:
        values = values * steps_of(stream_key, extent, cuts, -0.22, 0.18)
    return jnp.clip(values, -bound, bound).astype(kind)


def setup_inputs(seed: int = 0, part: int = 0) -> dict:
    key_list = jax.random.split(jax.random.key(seed), 10)
    own_keys = jax.random.split(jax.random.fold_in(key_list[9], part), 10)
    q_proj = centred(own_keys[0], (TOKENS, D), 1.0, 6.0, ((0, 8), (1, 2)))
    k_proj = centred(own_keys[1], (TOKENS, D), 1.0, 6.0, ((0, 8), (1, 2)))
    v_proj = centred(own_keys[2], (TOKENS, D), 1.0, 6.0, ((0, 8), (1, 2)))
    short_taps = centred(key_list[3], (3, SHORT, D), SHORT ** -0.5, 2.0, ((2, 2),))
    pole_rate = draw_pole_rate(jax.random.fold_in(key_list[9], 71), part)
    pole_angle = jnp.clip(jax.random.uniform(key_list[5], (M, D), jnp.float32, -3.140625, 3.140625), -3.140625, 3.140625)
    residue_re = draw_residue_re(jax.random.fold_in(key_list[9], 71), part)
    residue_im = draw_residue_im(jax.random.fold_in(key_list[9], 71), part)
    skip_gain = centred(key_list[8], (D,), 1.0, 3.0, ((0, 2),), jnp.float32)
    return dict(q_proj=q_proj, k_proj=k_proj, v_proj=v_proj, short_taps=short_taps, pole_rate=pole_rate, pole_angle=pole_angle, residue_re=residue_re, residue_im=residue_im, skip_gain=skip_gain)


def powers(rate, angle, steps):
    magnitude = jnp.exp(-rate[:, None, :] * steps[None, :, None])
    phase = angle[:, None, :] * steps[None, :, None]
    return magnitude * jnp.cos(phase), magnitude * jnp.sin(phase)


def complex_mul(first_re, first_im, second_re, second_im):
    return first_re * second_re - first_im * second_im, first_re * second_im + first_im * second_re


def short_conv(rows, taps):
    reach = taps.shape[0] - 1
    length = rows.shape[0]
    padded = jnp.concatenate([jnp.zeros((reach, rows.shape[1]), jnp.float32), rows.astype(jnp.float32)], axis=0)
    total = jnp.zeros((length, rows.shape[1]), jnp.float32)
    for offset in range(taps.shape[0]):
        total = total + taps[offset].astype(jnp.float32)[None, :] * padded[reach - offset:reach - offset + length]
    return total


def reference(q_proj, k_proj, v_proj, short_taps, pole_rate, pole_angle, residue_re, residue_im, skip_gain):
    block_len = TOK_DEV
    width = math.gcd(D, 512)
    col_blocks = D // width
    steps = jnp.arange(block_len).astype(jnp.float32)
    lags = jnp.arange(block_len).astype(jnp.int32)[:, None] - jnp.arange(block_len).astype(jnp.int32)[None, :]
    causal = lags >= 0
    lag_index = jnp.where(causal, lags, 0).astype(jnp.int32)

    def one_block(col_block):
        start = (col_block * width).astype(jnp.int32)

        def cols(array):
            return lax.dynamic_slice_in_dim(array, start, width, array.ndim - 1)

        rate, angle = cols(pole_rate), cols(pole_angle)
        res_re, res_im = cols(residue_re), cols(residue_im)
        taps = cols(short_taps)
        q_short = short_conv(cols(q_proj), taps[0])
        k_short = short_conv(cols(k_proj), taps[1])
        v_short = short_conv(cols(v_proj), taps[2])
        gated_f = (k_short * v_short).astype(jnp.bfloat16).astype(jnp.float32)
        van_re, van_im = powers(rate, angle, steps)
        filt = jnp.sum(res_re[:, None, :] * van_re - res_im[:, None, :] * van_im, axis=0)
        toeplitz = jnp.where(causal[:, :, None], filt[lag_index], jnp.float32(0.0))
        rev_re = van_re[:, ::-1, :]
        rev_im = van_im[:, ::-1, :]
        one_re, one_im = powers(rate, angle, jnp.ones((1,), jnp.float32))
        one_re, one_im = one_re[:, 0, :], one_im[:, 0, :]
        span_re, span_im = powers(rate, angle, jnp.full((1,), block_len, jnp.float32))
        span_re, span_im = span_re[:, 0, :], span_im[:, 0, :]
        gated_blocks = gated_f.reshape(N_SEQ, block_len, width)
        query_blocks = q_short.reshape(N_SEQ, block_len, width)

        def advance(carry, pieces):
            state_re, state_im = carry
            gated_rows, query_rows = pieces
            local_part = jnp.einsum("tsc,sc->tc", toeplitz, gated_rows, precision=lax.Precision.HIGHEST)
            lam_re, lam_im = complex_mul(one_re, one_im, state_re, state_im)
            coef_re, coef_im = complex_mul(res_re, res_im, lam_re, lam_im)
            carried = jnp.sum(coef_re[:, None, :] * van_re - coef_im[:, None, :] * van_im, axis=0)
            result = (query_rows * ((local_part + carried) + skip_gain_cols * gated_rows)).astype(jnp.bfloat16)
            end_re = jnp.sum(rev_re * gated_rows[None], axis=1)
            end_im = jnp.sum(rev_im * gated_rows[None], axis=1)
            decayed_re, decayed_im = complex_mul(span_re, span_im, state_re, state_im)
            return (decayed_re + end_re, decayed_im + end_im), result

        skip_gain_cols = cols(skip_gain)
        start_state = (jnp.zeros((M, width), jnp.float32), jnp.zeros((M, width), jnp.float32))
        unused, blocks = lax.scan(advance, start_state, (gated_blocks, query_blocks))
        return blocks.reshape(TOKENS, width)

    pieces = lax.map(one_block, jnp.arange(col_blocks).astype(jnp.int32))
    return jnp.transpose(pieces, (1, 0, 2)).reshape(TOKENS, D)
```

```python
import functools

import jax
import jax.numpy as jnp
from jax import lax
from jax.experimental import pallas as pl
from jax.experimental.pallas import tpu as pltpu
from jax.sharding import PartitionSpec as P

F32 = jnp.float32
BF16 = jnp.bfloat16
LANES = 128
ROWS = 8
CHUNK = 16

SIN = (0.9999999999829191, -0.16666666616793607, 0.008333330972826632,
       -0.00019840860946827691, 2.752525553710695e-06, -2.3888929551921256e-08)
COS = (0.9999999997792479, -0.4999999935536099, 0.04166663614859566,
       -0.0013888360060282819, 2.4760094764212313e-05, -2.605034249002706e-07)


def cmul(ar, ai, br, bi):
    return ar * br - ai * bi, ar * bi + ai * br


def horner(coefs, u):
    total = jnp.full_like(u, coefs[-1])
    for coef in coefs[-2::-1]:
        total = total * u + coef
    return total


def pole(rate, angle):
    half = angle * 0.5
    square = half * half
    sin_half = half * horner(SIN, square)
    cos_half = horner(COS, square)
    size = jnp.exp(-rate)
    return size * (1.0 - 2.0 * sin_half * sin_half), size * (2.0 * sin_half * cos_half)


def conv_rows(padded, taps, at, rows):
    total = None
    for j, tap in enumerate(taps):
        term = tap * padded[pl.ds(ROWS + at - j, rows), :]
        total = term if total is None else total + term
    return total


def fill(padded, rim, rows_in, first):
    padded[pl.ds(0, ROWS), :] = jnp.where(first, 0.0, rim.astype(F32))
    padded[pl.ds(ROWS, rows_in.shape[0]), :] = rows_in.astype(F32)


def tap_rows(ref, branch, lanes, scratch):
    count = ref.shape[1]
    scratch[pl.ds(0, count), :] = ref[branch, :, lanes].astype(F32)
    return [scratch[pl.ds(j, 1), :] for j in range(count)]


def over_tiles(width, body):
    def visit(i, carry):
        body(pl.ds(pl.multiple_of(i * LANES, LANES), LANES))
        return carry

    lax.fori_loop(0, width // LANES, visit, 0)


def state_kernel(info, k_ref, v_ref, rim_ref, taps_ref, rate_ref, angle_ref, res_re_ref, res_im_ref,
                 gated_ref, chunk_ref, total_ref, lam_ref, span_ref, filt_ref,
                 pad_k, pad_v, gate, tap_k, tap_v):
    first = info[1] == 1
    length, width = k_ref.shape
    chunks = length // CHUNK

    def tile(lanes):
        fill(pad_k, rim_ref[1, :, lanes], k_ref[:, lanes], first)
        fill(pad_v, rim_ref[2, :, lanes], v_ref[:, lanes], first)
        taps_k = tap_rows(taps_ref, 1, lanes, tap_k)
        taps_v = tap_rows(taps_ref, 2, lanes, tap_v)
        for at in range(0, length, CHUNK):
            product = conv_rows(pad_k, taps_k, at, CHUNK) * conv_rows(pad_v, taps_v, at, CHUNK)
            rounded = product.astype(BF16)
            gated_ref[pl.ds(at, CHUNK), lanes] = rounded
            gate[pl.ds(at, CHUNK), :] = rounded.astype(F32)
        lam_re, lam_im = pole(rate_ref[:, lanes], angle_ref[:, lanes])
        lam_ref[0, :, lanes] = lam_re
        lam_ref[1, :, lanes] = lam_im
        weight_re, weight_im = res_re_ref[:, lanes], res_im_ref[:, lanes]
        filt_ref[pl.ds(0, 1), lanes] = jnp.sum(weight_re, axis=0, keepdims=True)
        zero = jnp.zeros_like(weight_re)
        sums = [(zero, zero)] * chunks
        for b in range(CHUNK - 1, -1, -1):
            weight_re, weight_im = cmul(weight_re, weight_im, lam_re, lam_im)
            if b:
                filt_ref[pl.ds(CHUNK - b, 1), lanes] = jnp.sum(weight_re, axis=0, keepdims=True)
            for a in range(chunks):
                row = gate[pl.ds(a * CHUNK + b, 1), :]
                sums[a] = (sums[a][0] + weight_re * row, sums[a][1] + weight_im * row)
        step_re, step_im = lam_re, lam_im
        reach = 1
        while reach < CHUNK:
            step_re, step_im = cmul(step_re, step_im, step_re, step_im)
            reach *= 2
        total_re, total_im = sums[0]
        for a in range(chunks):
            chunk_ref[a, 0, :, lanes] = sums[a][0]
            chunk_ref[a, 1, :, lanes] = sums[a][1]
            if a:
                moved_re, moved_im = cmul(step_re, step_im, total_re, total_im)
                total_re, total_im = moved_re + sums[a][0], moved_im + sums[a][1]
        total_ref[0, :, lanes] = total_re
        total_ref[1, :, lanes] = total_im
        while reach < length:
            step_re, step_im = cmul(step_re, step_im, step_re, step_im)
            reach *= 2
        span_ref[0, :, lanes] = step_re
        span_ref[1, :, lanes] = step_im

    over_tiles(width, tile)


def local_kernel(info, q_ref, rim_ref, taps_ref, gain_ref, gated_ref, filt_ref,
                 query_ref, local_ref, pad_q, gate, tap_q):
    first = info[1] == 1
    length, width = q_ref.shape
    chunks = length // CHUNK
    gate[...] = jnp.zeros_like(gate)

    def tile(lanes):
        fill(pad_q, rim_ref[0, :, lanes], q_ref[:, lanes], first)
        taps = tap_rows(taps_ref, 0, lanes, tap_q)
        for at in range(0, length, CHUNK):
            query_ref[pl.ds(at, CHUNK), lanes] = conv_rows(pad_q, taps, at, CHUNK)
        for a in range(chunks):
            gate[pl.ds(2 * CHUNK * a + CHUNK, CHUNK), :] = gated_ref[pl.ds(a * CHUNK, CHUNK), lanes].astype(F32)
        filt = [filt_ref[pl.ds(j, 1), lanes] for j in range(CHUNK)]
        filt[0] = filt[0] + gain_ref[:, lanes]
        for a in range(chunks):
            base = 2 * CHUNK * a + CHUNK
            for low in range(0, CHUNK, ROWS):
                total = None
                for j in range(low + ROWS):
                    term = filt[j] * gate[pl.ds(base + low - j, ROWS), :]
                    total = term if total is None else total + term
                local_ref[pl.ds(a * CHUNK + low, ROWS), lanes] = total

    over_tiles(width, tile)


def carried_kernel(info, enter_ref, chunk_ref, lam_ref, query_ref, local_ref, *rest):
    out_ref, pow_re, pow_im, coef_re, coef_im = rest[-5:]
    length, width = query_ref.shape
    modes = lam_ref.shape[1]
    chunks = length // CHUNK

    def tile(lanes):
        lam_re, lam_im = lam_ref[0, :, lanes], lam_ref[1, :, lanes]
        now_re, now_im = jnp.ones_like(lam_re), jnp.zeros_like(lam_re)
        for b in range(CHUNK):
            pow_re[pl.ds(b * modes, modes), :] = now_re
            pow_im[pl.ds(b * modes, modes), :] = now_im
            now_re, now_im = cmul(now_re, now_im, lam_re, lam_im) if b else (lam_re, lam_im)
        state_re, state_im = enter_ref[0, :, lanes], enter_ref[1, :, lanes]
        for a in range(chunks):
            coef_re[pl.ds(a * modes, modes), :] = state_re
            coef_im[pl.ds(a * modes, modes), :] = state_im
            if a + 1 < chunks:
                state_re, state_im = cmul(now_re, now_im, state_re, state_im)
                state_re, state_im = state_re + chunk_ref[a, 0, :, lanes], state_im + chunk_ref[a, 1, :, lanes]
        totals = [local_ref[pl.ds(a * CHUNK, CHUNK), lanes] for a in range(chunks)]
        for m in range(modes):
            u_re = pow_re[pl.ds(m, CHUNK, stride=modes), :]
            u_im = pow_im[pl.ds(m, CHUNK, stride=modes), :]
            for a in range(chunks):
                c_re = coef_re[pl.ds(a * modes + m, 1), :]
                c_im = coef_im[pl.ds(a * modes + m, 1), :]
                totals[a] = totals[a] + (u_re * c_re - u_im * c_im)
        for a in range(chunks):
            at = pl.ds(a * CHUNK, CHUNK)
            out_ref[at, lanes] = (query_ref[at, lanes] * totals[a]).astype(BF16)

    over_tiles(width, tile)


def block_width(half):
    width = LANES
    while width < 512 and half % (2 * width) == 0:
        width *= 2
    return width


def shards(
    q_proj, k_proj, v_proj, short_taps, pole_rate, pole_angle, residue_re, residue_im, skip_gain
):
    length, channels = q_proj.shape
    branches, short_len = short_taps.shape[:2]
    modes = pole_rate.shape[0]
    half = channels // 2
    width = block_width(half)
    blocks = half // width
    chunks = length // CHUNK
    axis_size = lax.axis_size("seq")
    index = lax.axis_index("seq")
    odd = index % 2 == 1

    tails = jnp.stack([branch[length - ROWS:] for branch in (q_proj, k_proj, v_proj)])
    rims = lax.ppermute(tails, "seq", [(i, (i + 1) % axis_size) for i in range(axis_size)])
    is_first = (index == 0).astype(jnp.int32)
    own = (index % 2).astype(jnp.int32)
    gain = skip_gain[None]

    def at_half(shape):
        lead = len(shape) - 1
        return pl.BlockSpec(shape, lambda i, info: (0,) * lead + (info[0] * blocks + i,))

    def in_half(shape):
        lead = len(shape) - 1
        return pl.BlockSpec(shape, lambda i, info: (0,) * lead + (i,))

    def call(kernel, info, in_specs, out_specs, out_shape, scratch, cost, aliases=None):
        return pl.pallas_call(
            kernel,
            out_shape=out_shape,
            grid_spec=pltpu.PrefetchScalarGridSpec(
                num_scalar_prefetch=1, grid=(blocks,), in_specs=in_specs, out_specs=out_specs,
                scratch_shapes=scratch,
            ),
            input_output_aliases=aliases or {},
            cost_estimate=pl.CostEstimate(flops=cost, bytes_accessed=cost, transcendentals=0),
        )

    def vmem(rows):
        return pltpu.VMEM((rows, LANES), F32)

    def shape(*dims, dtype=F32):
        return jax.ShapeDtypeStruct(dims, dtype)

    def states(info):
        return call(
            state_kernel,
            info,
            [at_half((length, width))] * 2
            + [at_half((branches, ROWS, width)), at_half((branches, short_len, width))]
            + [at_half((modes, width))] * 4,
            [in_half((length, width)), in_half((chunks, 2, modes, width))]
            + [in_half((2, modes, width))] * 3 + [in_half((CHUNK, width))],
            [shape(length, half, dtype=BF16), shape(chunks, 2, modes, half)]
            + [shape(2, modes, half)] * 3 + [shape(CHUNK, half)],
            [vmem(length + ROWS), vmem(length + ROWS), vmem(length), vmem(ROWS), vmem(ROWS)],
            1 << 20,
        )(info, k_proj, v_proj, rims, short_taps, pole_rate, pole_angle, residue_re, residue_im)

    def local(info, gated, filt):
        return call(
            local_kernel,
            info,
            [at_half((length, width)), at_half((branches, ROWS, width)), at_half((branches, short_len, width)),
             at_half((1, width)), in_half((length, width)), in_half((CHUNK, width))],
            [in_half((length, width))] * 2,
            [shape(length, half)] * 2,
            [vmem(length + ROWS), vmem(2 * length), vmem(ROWS)],
            1 << 20,
        )(info, q_proj, rims, short_taps, gain, gated, filt)

    def finish(info, enter, chunk, lam, query, near, out=None):
        args = [info, enter, chunk, lam, query, near]
        specs = [in_half((2, modes, width)), in_half((chunks, 2, modes, width)), in_half((2, modes, width)),
                 in_half((length, width)), in_half((length, width))]
        aliases = None
        if out is not None:
            args.append(out)
            specs.append(pl.BlockSpec(memory_space=pl.ANY))
            aliases = {len(args) - 1: 0}
        return call(
            carried_kernel, info, specs, at_half((length, width)), shape(length, channels, dtype=BF16),
            [vmem(CHUNK * modes), vmem(CHUNK * modes), vmem(chunks * modes), vmem(chunks * modes)],
            1 << 20, aliases,
        )(*args)

    def swap(block, distance):
        return lax.ppermute(block, "seq", [(i, i ^ distance) for i in range(axis_size)])

    def times(a, b):
        return jnp.stack(cmul(a[0], a[1], b[0], b[1]))

    info_own = jnp.stack([own, is_first])
    info_other = jnp.stack([1 - own, is_first])
    gated_o, chunk_o, total_o, lam_o, _, filt_o = states(info_other)
    from_mate = swap(total_o.astype(BF16), 1)
    gated_m, chunk_m, total_m, lam_m, span, filt_m = states(info_own)
    query_o, near_o = local(info_other, gated_o, filt_o)
    query_m, near_m = local(info_own, gated_m, filt_m)

    from_mate = from_mate.astype(F32)
    early = jnp.where(odd, from_mate, total_m)
    late = jnp.where(odd, total_m, from_mate)
    block = times(span, early) + late
    power = times(span, span)
    enter = jnp.zeros_like(block)
    decay = None
    distance = 2
    while distance < axis_size:
        arrived = swap(block.astype(BF16), distance).astype(F32)
        upper = (index & distance) != 0
        moved = arrived if decay is None else times(decay, arrived)
        enter = enter + jnp.where(upper, moved, 0.0)
        if 2 * distance < axis_size:
            block = times(power, jnp.where(upper, arrived, block)) + jnp.where(upper, block, arrived)
            one = jnp.stack([jnp.ones_like(power[0]), jnp.zeros_like(power[0])])
            grown = jnp.where(upper, power, one)
            decay = grown if decay is None else times(decay, grown)
            power = times(power, power)
        distance *= 2
    past = times(span, enter) + early
    handed = swap(jnp.where(odd, enter, past).astype(BF16), 1)
    mine = jnp.where(odd, past, enter)
    out = finish(info_own, mine, chunk_m, lam_m, query_m, near_m)
    return finish(info_other, handed.astype(F32), chunk_o, lam_o, query_o, near_o, out)


def solution(mesh):
    placed = (
        P(("groups", "seq"), "tensor"),
        P(("groups", "seq"), "tensor"),
        P(("groups", "seq"), "tensor"),
        P(None, None, "tensor"),
        P(None, "tensor"),
        P(None, "tensor"),
        P(None, "tensor"),
        P(None, "tensor"),
        P("tensor"),
    )
    return jax.shard_map(
        shards,
        mesh=mesh,
        in_specs=placed,
        out_specs=P(("groups", "seq"), "tensor"),
        check_vma=False,
    )
```

```python
import functools
import math

import jax
import jax.numpy as jnp
from jax import lax
from jax.experimental import pallas as pl
from jax.experimental.pallas import tpu as pltpu
from jax.sharding import PartitionSpec as P

F32 = jnp.float32
BF16 = jnp.bfloat16
LANES = 128
ROWS = 8
CHUNK = 16

SIN = (0.9999999999829191, -0.16666666616793607, 0.008333330972826632,
       -0.00019840860946827691, 2.752525553710695e-06, -2.3888929551921256e-08)
COS = (0.9999999997792479, -0.4999999935536099, 0.04166663614859566,
       -0.0013888360060282819, 2.4760094764212313e-05, -2.605034249002706e-07)


def cmul(ar, ai, br, bi):
    return ar * br - ai * bi, ar * bi + ai * br


def horner(coefs, u):
    total = jnp.full_like(u, coefs[-1])
    for coef in coefs[-2::-1]:
        total = total * u + coef
    return total


def pole(rate, angle):
    half = angle * 0.5
    square = half * half
    sin_half = half * horner(SIN, square)
    cos_half = horner(COS, square)
    size = jnp.exp(-rate)
    return size * (1.0 - 2.0 * sin_half * sin_half), size * (2.0 * sin_half * cos_half)


def conv_rows(padded, taps, at, rows):
    total = None
    for j, tap in enumerate(taps):
        term = tap * padded[pl.ds(ROWS + at - j, rows), :]
        total = term if total is None else total + term
    return total


def tap_rows(ref, branch, lanes, scratch):
    count = ref.shape[1]
    scratch[pl.ds(0, count), :] = ref[branch, :, lanes].astype(F32)
    return [scratch[pl.ds(j, 1), :] for j in range(count)]


def aligned(start):
    return pl.ds(pl.multiple_of(start, LANES), LANES)


def over_tiles(width, base, body):
    def visit(i, carry):
        body(aligned(base + i * LANES), aligned(i * LANES))
        return carry

    lax.fori_loop(0, width // LANES, visit, 0)


def half_start(width, mine):
    index = lax.axis_index("seq")
    parity = lax.rem(index, 2)
    return index == 0, (parity if mine else 1 - parity) * width


def power_of(re, im, doublings):
    for _ in range(doublings):
        re, im = cmul(re, im, re, im)
    return re, im


def gate_rows(pad_k, pad_v, taps_k, taps_v, at, gated_ref, lanes, gate):
    product = conv_rows(pad_k, taps_k, at, CHUNK) * conv_rows(pad_v, taps_v, at, CHUNK)
    rounded = product.astype(BF16)
    gated_ref[pl.ds(at, CHUNK), lanes] = rounded
    gate[pl.ds(at, CHUNK), :] = rounded.astype(F32)


def chunk_sums(gate, chunks, lam_re, lam_im):
    twice = lam_re + lam_re
    square = lam_re * lam_re + lam_im * lam_im
    older, newer = [None] * len(chunks), [None] * len(chunks)
    for b in range(CHUNK):
        for n, a in enumerate(chunks):
            now = gate[pl.ds(a * CHUNK + b, 1), :]
            if b == 0:
                now = jnp.broadcast_to(now, lam_re.shape)
            if b > 1:
                now = now - square * older[n]
            if b > 0:
                now = now + twice * newer[n]
            older[n], newer[n] = newer[n], now
    return [(new - lam_re * old, lam_im * old) for old, new in zip(older, newer)]


def put(ref, lanes, pair, *at):
    ref[(*at, 0, slice(None), lanes)] = pair[0].astype(ref.dtype)
    ref[(*at, 1, slice(None), lanes)] = pair[1].astype(ref.dtype)


def get(ref, lanes, *at):
    return ref[(*at, 0, slice(None), lanes)].astype(F32), ref[(*at, 1, slice(None), lanes)].astype(F32)


def add(a, b):
    return a[0] + b[0], a[1] + b[1]


def states_kernel(with_rim, *refs):
    refs = list(refs)
    k_ref, v_ref = refs[:2]
    rim_ref = refs.pop(2) if with_rim else None
    taps_ref, rate_ref, angle_ref = refs[2:5]
    gated_ref, chunk_ref, total_ref, lam_ref, step_ref, span_ref, pad_k, pad_v, gate, tap_k, tap_v = refs[5:]
    length = k_ref.shape[0]
    width = gated_ref.shape[1]
    first, base = half_start(width, with_rim)
    chunks = list(range(0 if with_rim else 1, length // CHUNK))

    def tile(full, half):
        for pad, ref, branch in ((pad_k, k_ref, 1), (pad_v, v_ref, 2)):
            if with_rim:
                pad[pl.ds(0, ROWS), :] = jnp.where(first, 0.0, rim_ref[branch, :, full].astype(F32))
            pad[pl.ds(ROWS, length), :] = ref[:, full].astype(F32)
        taps_k = tap_rows(taps_ref, 1, full, tap_k)
        taps_v = tap_rows(taps_ref, 2, full, tap_v)
        for a in chunks:
            gate_rows(pad_k, pad_v, taps_k, taps_v, a * CHUNK, gated_ref, half, gate)
        lam = pole(rate_ref[:, full], angle_ref[:, full])
        put(lam_ref, half, lam)
        sums = chunk_sums(gate, chunks, *lam)
        step = power_of(*lam, CHUNK.bit_length() - 1)
        put(step_ref, half, step)
        total = sums[0]
        for a, chunk in zip(chunks, sums):
            put(chunk_ref, half, chunk, a)
            if a != chunks[0]:
                total = add(cmul(*step, *total), chunk)
        put(total_ref, half, total)
        if with_rim:
            put(span_ref, half, power_of(*step, (length // CHUNK).bit_length() - 1))
        else:
            far, grown = None, step
            count = length // CHUNK - 1
            while count:
                if count % 2:
                    far = grown if far is None else cmul(*far, *grown)
                count //= 2
                if count:
                    grown = cmul(*grown, *grown)
            put(span_ref, half, far)

    over_tiles(width, base, tile)


def head_kernel(k_ref, v_ref, rim_ref, taps_ref, lam_ref, far_ref, rest_ref, gated_in, chunk_in,
                gated_ref, chunk_ref, total_ref, pad_k, pad_v, gate, tap_k, tap_v):
    del gated_in, chunk_in
    width = gated_ref.shape[1]
    first, base = half_start(width, False)

    def tile(full, half):
        for pad, ref, branch in ((pad_k, k_ref, 1), (pad_v, v_ref, 2)):
            pad[pl.ds(0, ROWS), :] = jnp.where(first, 0.0, rim_ref[branch, :, full].astype(F32))
            pad[pl.ds(ROWS, CHUNK), :] = ref[pl.ds(0, CHUNK), full].astype(F32)
        taps_k = tap_rows(taps_ref, 1, full, tap_k)
        taps_v = tap_rows(taps_ref, 2, full, tap_v)
        gate_rows(pad_k, pad_v, taps_k, taps_v, 0, gated_ref, half, gate)
        (chunk,) = chunk_sums(gate, [0], *get(lam_ref, half))
        put(chunk_ref, half, chunk, 0)
        put(total_ref, half, add(get(rest_ref, half), cmul(*get(far_ref, half), *chunk)))

    over_tiles(width, base, tile)


def local_kernel(mine, q_ref, rim_ref, taps_ref, gain_ref, res_re_ref, res_im_ref, lam_ref, gated_ref,
                 query_ref, local_ref, pow_ref, pad_q, gate, tap_q, table_re, table_im, line, mix):
    length = q_ref.shape[0]
    width = gated_ref.shape[1]
    modes = lam_ref.shape[1]
    first, base = half_start(width, mine)
    chunks = length // CHUNK
    side = ROWS // 2
    groups = modes // side
    for a in range(chunks):
        gate[pl.ds(2 * CHUNK * a, CHUNK), :] = jnp.zeros((CHUNK, LANES), F32)

    def tile(full, half):
        pad_q[pl.ds(0, ROWS), :] = jnp.where(first, 0.0, rim_ref[0, :, full].astype(F32))
        pad_q[pl.ds(ROWS, length), :] = q_ref[:, full].astype(F32)
        taps = tap_rows(taps_ref, 0, full, tap_q)
        for at in range(0, length, CHUNK):
            query_ref[pl.ds(at, CHUNK), half] = conv_rows(pad_q, taps, at, CHUNK)
        for a in range(chunks):
            gate[pl.ds(2 * CHUNK * a + CHUNK, CHUNK), :] = gated_ref[pl.ds(a * CHUNK, CHUNK), half].astype(F32)
        lam = get(lam_ref, half)
        res = res_re_ref[:, full], res_im_ref[:, full]
        even = cmul(*res, *lam)
        odd = cmul(*even, *lam)
        two = cmul(*lam, *lam)
        for n, part in enumerate((*even, *odd, *two)):
            line[pl.ds(n * modes, modes), :] = part
        for g in range(groups):
            for n, sources in enumerate(((0, 2), (1, 3), (4, 4), (5, 5))):
                for m, source in enumerate(sources):
                    at = (n * groups + g) * ROWS + m * side
                    mix[pl.ds(at, side), :] = line[pl.ds(source * modes + g * side, side), :]
        for g in range(groups):
            now_re, now_im, by_re, by_im = (mix[pl.ds((n * groups + g) * ROWS, ROWS), :] for n in range(4))
            for j in range(0, CHUNK, 2):
                at = pl.ds((g * CHUNK + j) * side, ROWS)
                table_re[at, :] = now_re
                table_im[at, :] = now_im
                if j + 2 < CHUNK:
                    now_re, now_im = cmul(now_re, now_im, by_re, by_im)
        later = None
        for m in range(modes):
            at = pl.ds(m // side * CHUNK * side + m % side, CHUNK, stride=side)
            u_re = table_re[at, :]
            pow_ref[0, m, :, half] = u_re
            pow_ref[1, m, :, half] = table_im[at, :]
            later = u_re if later is None else later + u_re
        line[pl.ds(0, CHUNK), :] = later
        filt = [jnp.sum(res[0], axis=0, keepdims=True) + gain_ref[:, full]]
        filt += [line[pl.ds(j, 1), :] for j in range(CHUNK - 1)]
        filt[0] = jnp.broadcast_to(filt[0], (ROWS, LANES))
        for a in range(chunks):
            start = 2 * CHUNK * a + CHUNK
            for low in range(0, CHUNK, ROWS):
                total = None
                for j in range(low + ROWS):
                    term = filt[j] * gate[pl.ds(start + low - j, ROWS), :]
                    total = term if total is None else total + term
                local_ref[pl.ds(a * CHUNK + low, ROWS), half] = total

    over_tiles(width, base, tile)


def carried_kernel(mine, enter_ref, chunk_ref, step_ref, pow_ref, query_ref, local_ref, *rest):
    out_ref, coef_re, coef_im, stage, sems = rest[-5:]
    length, width = query_ref.shape
    modes = step_ref.shape[1]
    chunks = length // CHUNK
    base = half_start(width, mine)[1]
    pieces = sems.shape[0]
    span = width // pieces

    def tile(half):
        step = get(step_ref, half)
        state = get(enter_ref, half)
        for a in range(chunks):
            coef_re[pl.ds(a * modes, modes), :] = state[0]
            coef_im[pl.ds(a * modes, modes), :] = state[1]
            if a + 1 < chunks:
                state = add(cmul(*step, *state), get(chunk_ref, half, a))
        totals = [local_ref[pl.ds(a * CHUNK, CHUNK), half] for a in range(chunks)]
        for m in range(modes):
            u_re = pow_ref[0, m, :, half]
            u_im = pow_ref[1, m, :, half]
            for a in range(chunks):
                c_re = coef_re[pl.ds(a * modes + m, 1), :]
                c_im = coef_im[pl.ds(a * modes + m, 1), :]
                totals[a] = totals[a] + (u_re * c_re - u_im * c_im)
        for a in range(chunks):
            at = pl.ds(a * CHUNK, CHUNK)
            stage[at, half] = (query_ref[at, half] * totals[a]).astype(BF16)

    def copy(piece):
        here = pl.ds(pl.multiple_of(piece * span, LANES), span)
        there = pl.ds(pl.multiple_of(base + piece * span, LANES), span)
        return pltpu.make_async_copy(stage.at[:, here], out_ref.at[:, there], sems.at[piece])

    def visit(piece, carry):
        def inner(i, carry):
            tile(aligned(piece * span + i * LANES))
            return carry

        lax.fori_loop(0, span // LANES, inner, 0)
        copy(piece).start()
        return carry

    lax.fori_loop(0, pieces, visit, 0)
    for piece in range(pieces):
        copy(piece).wait()


def tails_kernel(*refs):
    count = (len(refs) - 2) // 1
    sources, out_ref, sems = refs[:count], refs[count], refs[count + 1]
    copies = [
        pltpu.make_async_copy(ref.at[pl.ds(ref.shape[0] - ROWS, ROWS), :], out_ref.at[n], sems.at[n])
        for n, ref in enumerate(sources)
    ]
    for copy in copies:
        copy.start()
    for copy in copies:
        copy.wait()


def shards(
    q_proj, k_proj, v_proj, short_taps, pole_rate, pole_angle, residue_re, residue_im, skip_gain
):
    length, channels = q_proj.shape
    branches, short_len = short_taps.shape[:2]
    modes = pole_rate.shape[0]
    half = channels // 2
    chunks = length // CHUNK
    axis_size = lax.axis_size("seq")
    index = lax.axis_index("seq")
    odd = index % 2 == 1
    inside = pl.BlockSpec(memory_space=pltpu.VMEM)
    outside = pl.BlockSpec(memory_space=pl.ANY)

    def near(array):
        return pltpu.with_memory_space_constraint(array, pltpu.VMEM)

    def call(kernel, args, outs, scratch, cost, aliases=None, in_specs=None, out_specs=None):
        return pl.pallas_call(
            kernel,
            out_shape=outs,
            in_specs=in_specs or [inside] * len(args),
            out_specs=out_specs or ([inside] * len(outs) if isinstance(outs, list) else inside),
            scratch_shapes=scratch,
            input_output_aliases=aliases or {},
            compiler_params=pltpu.CompilerParams(vmem_limit_bytes=4 << 20),
            cost_estimate=pl.CostEstimate(flops=cost, bytes_accessed=cost, transcendentals=0),
        )(*args)

    def rows(count):
        return pltpu.VMEM((count, LANES), F32)

    def modal(dtype=F32):
        return pltpu.VMEM((2, modes, half), dtype)

    def swap(block, distance):
        return lax.ppermute(block, "seq", [(i, i ^ distance) for i in range(axis_size)])

    def times(a, b):
        return jnp.stack(cmul(a[0], a[1], b[0], b[1]))

    gates = pltpu.VMEM((length, half), BF16)
    sums = pltpu.VMEM((chunks, 2, modes, half), F32)
    pads = [rows(length + ROWS), rows(length + ROWS), rows(length), rows(ROWS), rows(ROWS)]

    tails = call(
        tails_kernel, [q_proj, k_proj, v_proj], pltpu.VMEM((branches, ROWS, channels), q_proj.dtype),
        [pltpu.SemaphoreType.DMA((branches,))], 1 << 16, in_specs=[outside] * branches,
    )
    rims = lax.ppermute(tails, "seq", [(i, (i + 1) % axis_size) for i in range(axis_size)])
    q, k, v, taps, rate, angle, res_re, res_im, gain = (
        near(array) for array in (
            q_proj, k_proj, v_proj, short_taps, pole_rate, pole_angle, residue_re, residue_im, skip_gain[None]
        )
    )

    gated_o, chunk_o, rest_o, lam_o, step_o, far_o = call(
        functools.partial(states_kernel, False), [k, v, taps, rate, angle],
        [gates, sums, modal(), modal(), modal(), modal()], pads, 16 << 20,
    )
    gated_o, chunk_o, total_o = call(
        head_kernel, [k, v, near(rims), taps, near(lam_o), near(far_o), near(rest_o), near(gated_o), near(chunk_o)],
        [gates, sums, modal(BF16)],
        [rows(CHUNK + ROWS), rows(CHUNK + ROWS), rows(CHUNK), rows(ROWS), rows(ROWS)],
        2 << 20, aliases={7: 0, 8: 1},
    )
    from_mate = swap(total_o, 1)
    gated_m, chunk_m, total_m, lam_m, step_m, span = call(
        functools.partial(states_kernel, True), [k, v, near(rims), taps, rate, angle],
        [gates, sums, modal(), modal(), modal(), modal()], pads, 16 << 20,
    )

    def local(mine, lam, gated):
        return call(
            functools.partial(local_kernel, mine),
            [q, near(rims), taps, gain, res_re, res_im, near(lam), near(gated)],
            [pltpu.VMEM((length, half), F32), pltpu.VMEM((length, half), F32), pltpu.VMEM((2, modes, CHUNK, half), F32)],
            [rows(length + ROWS), rows(2 * length), rows(ROWS), rows(CHUNK * modes), rows(CHUNK * modes),
             rows(6 * modes), rows(8 * modes)],
            8 << 20,
        )

    def finish(mine, enter, chunk, step, made, out=None):
        query, close, power = made
        args = [near(array) for array in (enter, chunk, step, power, query, close)]
        specs = [inside] * len(args)
        aliases = None
        if out is not None:
            args.append(out)
            specs.append(outside)
            aliases = {len(args) - 1: 0}
        pieces = math.gcd(half // LANES, 4)
        return call(
            functools.partial(carried_kernel, mine), args, jax.ShapeDtypeStruct((length, channels), BF16),
            [rows(chunks * modes), rows(chunks * modes), pltpu.VMEM((length, half), BF16),
             pltpu.SemaphoreType.DMA((pieces,))],
            8 << 20, aliases, specs, outside,
        )

    from_mate = from_mate.astype(F32)
    early = jnp.where(odd, from_mate, total_m)
    late = jnp.where(odd, total_m, from_mate)
    block = times(span, early) + late
    made_o = local(False, lam_o, gated_o)
    made_m = None
    power = times(span, span)
    enter = jnp.zeros_like(block)
    decay = None
    distance = 2
    while distance < axis_size:
        arrived = swap(block.astype(BF16), distance).astype(F32)
        upper = (index & distance) != 0
        moved = arrived if decay is None else times(decay, arrived)
        enter = enter + jnp.where(upper, moved, 0.0)
        if 2 * distance < axis_size:
            block = times(power, jnp.where(upper, arrived, block)) + jnp.where(upper, block, arrived)
            one = jnp.stack([jnp.ones_like(power[0]), jnp.zeros_like(power[0])])
            grown = jnp.where(upper, power, one)
            decay = grown if decay is None else times(decay, grown)
            power = times(power, power)
            if made_m is None:
                gated_m, block = lax.optimization_barrier((gated_m, block))
                made_m = local(True, lam_m, gated_m)
        distance *= 2
    if made_m is None:
        made_m = local(True, lam_m, gated_m)
    past = times(span, enter) + early
    handed = swap(jnp.where(odd, enter, past).astype(BF16), 1)
    mine = jnp.where(odd, past, enter)
    out = finish(True, mine, chunk_m, step_m, made_m)
    return finish(False, handed, chunk_o, step_o, made_o, out)


def solution(mesh):
    placed = (
        P(("groups", "seq"), "tensor"),
        P(("groups", "seq"), "tensor"),
        P(("groups", "seq"), "tensor"),
        P(None, None, "tensor"),
        P(None, "tensor"),
        P(None, "tensor"),
        P(None, "tensor"),
        P(None, "tensor"),
        P("tensor"),
    )
    return jax.shard_map(
        shards,
        mesh=mesh,
        in_specs=placed,
        out_specs=P(("groups", "seq"), "tensor"),
        check_vma=False,
    )
```

```python
import functools
import math

import jax
import jax.numpy as jnp
from jax import lax
from jax.experimental import pallas as pl
from jax.experimental.pallas import tpu as pltpu
from jax.sharding import PartitionSpec as P

F32 = jnp.float32
BF16 = jnp.bfloat16
LANES = 128
ROWS = 8
CHUNK = 16

SIN = (0.9999999999829191, -0.16666666616793607, 0.008333330972826632,
       -0.00019840860946827691, 2.752525553710695e-06, -2.3888929551921256e-08)
COS = (0.9999999997792479, -0.4999999935536099, 0.04166663614859566,
       -0.0013888360060282819, 2.4760094764212313e-05, -2.605034249002706e-07)


def cmul(ar, ai, br, bi):
    return ar * br - ai * bi, ar * bi + ai * br


def horner(coefs, u):
    total = jnp.full_like(u, coefs[-1])
    for coef in coefs[-2::-1]:
        total = total * u + coef
    return total


def pole(rate, angle):
    half = angle * 0.5
    square = half * half
    sin_half = half * horner(SIN, square)
    cos_half = horner(COS, square)
    size = jnp.exp(-rate)
    return size * (1.0 - 2.0 * sin_half * sin_half), size * (2.0 * sin_half * cos_half)


def conv_rows(padded, taps, at, rows):
    total = None
    for j, tap in enumerate(taps):
        term = tap * padded[pl.ds(ROWS + at - j, rows), :]
        total = term if total is None else total + term
    return total


def tap_rows(ref, branch, lanes, scratch):
    count = ref.shape[1]
    scratch[pl.ds(0, count), :] = ref[branch, :, lanes].astype(F32)
    return [scratch[pl.ds(j, 1), :] for j in range(count)]


def aligned(start):
    return pl.ds(pl.multiple_of(start, LANES), LANES)


def over_tiles(width, base, body):
    def visit(i, carry):
        body(aligned(base + i * LANES), aligned(i * LANES))
        return carry

    lax.fori_loop(0, width // LANES, visit, 0)


def half_start(width, mine):
    index = lax.axis_index("seq")
    parity = lax.rem(index, 2)
    return index == 0, (parity if mine else 1 - parity) * width


def power_of(re, im, doublings):
    for _ in range(doublings):
        re, im = cmul(re, im, re, im)
    return re, im


def gate_rows(pad_k, pad_v, taps_k, taps_v, at, gated_ref, lanes, gate):
    product = conv_rows(pad_k, taps_k, at, CHUNK) * conv_rows(pad_v, taps_v, at, CHUNK)
    rounded = product.astype(BF16)
    gated_ref[pl.ds(at, CHUNK), lanes] = rounded
    gate[pl.ds(at, CHUNK), :] = rounded.astype(F32)


def chunk_sums(gate, chunks, lam_re, lam_im):
    twice = lam_re + lam_re
    square = lam_re * lam_re + lam_im * lam_im
    older, newer = [None] * len(chunks), [None] * len(chunks)
    for b in range(CHUNK):
        for n, a in enumerate(chunks):
            now = gate[pl.ds(a * CHUNK + b, 1), :]
            if b == 0:
                now = jnp.broadcast_to(now, lam_re.shape)
            if b > 1:
                now = now - square * older[n]
            if b > 0:
                now = now + twice * newer[n]
            older[n], newer[n] = newer[n], now
    return [(new - lam_re * old, lam_im * old) for old, new in zip(older, newer)]


def put(ref, lanes, pair, *at):
    ref[(*at, 0, slice(None), lanes)] = pair[0].astype(ref.dtype)
    ref[(*at, 1, slice(None), lanes)] = pair[1].astype(ref.dtype)


def get(ref, lanes, *at):
    return ref[(*at, 0, slice(None), lanes)].astype(F32), ref[(*at, 1, slice(None), lanes)].astype(F32)


def add(a, b):
    return a[0] + b[0], a[1] + b[1]


def states_kernel(with_rim, *refs):
    refs = list(refs)
    k_ref, v_ref = refs[:2]
    rim_ref = refs.pop(2) if with_rim else None
    taps_ref, rate_ref, angle_ref = refs[2:5]
    gated_ref, chunk_ref, total_ref, lam_ref, step_ref, span_ref, pad_k, pad_v, gate, tap_k, tap_v = refs[5:]
    length = k_ref.shape[0]
    width = gated_ref.shape[1]
    first, base = half_start(width, with_rim)
    chunks = list(range(0 if with_rim else 1, length // CHUNK))

    def tile(full, half):
        for pad, ref, branch in ((pad_k, k_ref, 1), (pad_v, v_ref, 2)):
            if with_rim:
                pad[pl.ds(0, ROWS), :] = jnp.where(first, 0.0, rim_ref[branch, :, full].astype(F32))
            pad[pl.ds(ROWS, length), :] = ref[:, full].astype(F32)
        taps_k = tap_rows(taps_ref, 1, full, tap_k)
        taps_v = tap_rows(taps_ref, 2, full, tap_v)
        for a in chunks:
            gate_rows(pad_k, pad_v, taps_k, taps_v, a * CHUNK, gated_ref, half, gate)
        lam = pole(rate_ref[:, full], angle_ref[:, full])
        put(lam_ref, half, lam)
        sums = chunk_sums(gate, chunks, *lam)
        step = power_of(*lam, CHUNK.bit_length() - 1)
        put(step_ref, half, step)
        total = sums[0]
        for a, chunk in zip(chunks, sums):
            put(chunk_ref, half, chunk, a)
            if a != chunks[0]:
                total = add(cmul(*step, *total), chunk)
        put(total_ref, half, total)
        if with_rim:
            put(span_ref, half, power_of(*step, (length // CHUNK).bit_length() - 1))
        else:
            far, grown = None, step
            count = length // CHUNK - 1
            while count:
                if count % 2:
                    far = grown if far is None else cmul(*far, *grown)
                count //= 2
                if count:
                    grown = cmul(*grown, *grown)
            put(span_ref, half, far)

    over_tiles(width, base, tile)


def head_kernel(k_ref, v_ref, rim_ref, taps_ref, lam_ref, far_ref, rest_ref, gated_in, chunk_in,
                gated_ref, chunk_ref, total_ref, pad_k, pad_v, gate, tap_k, tap_v):
    del gated_in, chunk_in
    width = gated_ref.shape[1]
    first, base = half_start(width, False)

    def tile(full, half):
        for pad, ref, branch in ((pad_k, k_ref, 1), (pad_v, v_ref, 2)):
            pad[pl.ds(0, ROWS), :] = jnp.where(first, 0.0, rim_ref[branch, :, full].astype(F32))
            pad[pl.ds(ROWS, CHUNK), :] = ref[pl.ds(0, CHUNK), full].astype(F32)
        taps_k = tap_rows(taps_ref, 1, full, tap_k)
        taps_v = tap_rows(taps_ref, 2, full, tap_v)
        gate_rows(pad_k, pad_v, taps_k, taps_v, 0, gated_ref, half, gate)
        (chunk,) = chunk_sums(gate, [0], *get(lam_ref, half))
        put(chunk_ref, half, chunk, 0)
        put(total_ref, half, add(get(rest_ref, half), cmul(*get(far_ref, half), *chunk)))

    over_tiles(width, base, tile)


def local_kernel(mine, after_ref, q_ref, rim_ref, taps_ref, gain_ref, res_re_ref, res_im_ref, lam_ref, gated_ref,
                 query_ref, local_ref, pow_ref, pad_q, gate, tap_q, table_re, table_im, line, mix):
    length = q_ref.shape[0]
    width = gated_ref.shape[1]
    modes = lam_ref.shape[1]
    del after_ref
    first, base = half_start(width, mine)
    chunks = length // CHUNK
    side = ROWS // 2
    groups = modes // side
    for a in range(chunks):
        gate[pl.ds(2 * CHUNK * a, CHUNK), :] = jnp.zeros((CHUNK, LANES), F32)

    def tile(full, half):
        pad_q[pl.ds(0, ROWS), :] = jnp.where(first, 0.0, rim_ref[0, :, full].astype(F32))
        pad_q[pl.ds(ROWS, length), :] = q_ref[:, full].astype(F32)
        taps = tap_rows(taps_ref, 0, full, tap_q)
        for at in range(0, length, CHUNK):
            query_ref[pl.ds(at, CHUNK), half] = conv_rows(pad_q, taps, at, CHUNK)
        for a in range(chunks):
            gate[pl.ds(2 * CHUNK * a + CHUNK, CHUNK), :] = gated_ref[pl.ds(a * CHUNK, CHUNK), half].astype(F32)
        lam = get(lam_ref, half)
        res = res_re_ref[:, full], res_im_ref[:, full]
        even = cmul(*res, *lam)
        odd = cmul(*even, *lam)
        two = cmul(*lam, *lam)
        for n, part in enumerate((*even, *odd, *two)):
            line[pl.ds(n * modes, modes), :] = part
        for g in range(groups):
            for n, sources in enumerate(((0, 2), (1, 3), (4, 4), (5, 5))):
                for m, source in enumerate(sources):
                    at = (n * groups + g) * ROWS + m * side
                    mix[pl.ds(at, side), :] = line[pl.ds(source * modes + g * side, side), :]
        for g in range(groups):
            now_re, now_im, by_re, by_im = (mix[pl.ds((n * groups + g) * ROWS, ROWS), :] for n in range(4))
            for j in range(0, CHUNK, 2):
                at = pl.ds((g * CHUNK + j) * side, ROWS)
                table_re[at, :] = now_re
                table_im[at, :] = now_im
                if j + 2 < CHUNK:
                    now_re, now_im = cmul(now_re, now_im, by_re, by_im)
        later = None
        for m in range(modes):
            at = pl.ds(m // side * CHUNK * side + m % side, CHUNK, stride=side)
            u_re = table_re[at, :]
            pow_ref[0, m, :, half] = u_re
            pow_ref[1, m, :, half] = table_im[at, :]
            later = u_re if later is None else later + u_re
        line[pl.ds(0, CHUNK), :] = later
        filt = [jnp.sum(res[0], axis=0, keepdims=True) + gain_ref[:, full]]
        filt += [line[pl.ds(j, 1), :] for j in range(CHUNK - 1)]
        filt[0] = jnp.broadcast_to(filt[0], (ROWS, LANES))
        for a in range(chunks):
            start = 2 * CHUNK * a + CHUNK
            for low in range(0, CHUNK, ROWS):
                total = None
                for j in range(low + ROWS):
                    term = filt[j] * gate[pl.ds(start + low - j, ROWS), :]
                    total = term if total is None else total + term
                local_ref[pl.ds(a * CHUNK + low, ROWS), half] = total

    over_tiles(width, base, tile)


def carried_kernel(mine, enter_ref, chunk_ref, step_ref, pow_ref, query_ref, local_ref, *rest):
    out_ref, coef_re, coef_im, stage, sems = rest[-5:]
    length, width = query_ref.shape
    modes = step_ref.shape[1]
    chunks = length // CHUNK
    base = half_start(width, mine)[1]
    pieces = sems.shape[0]
    span = width // pieces

    def tile(half):
        step = get(step_ref, half)
        state = get(enter_ref, half)
        for a in range(chunks):
            coef_re[pl.ds(a * modes, modes), :] = state[0]
            coef_im[pl.ds(a * modes, modes), :] = state[1]
            if a + 1 < chunks:
                state = add(cmul(*step, *state), get(chunk_ref, half, a))
        totals = [local_ref[pl.ds(a * CHUNK, CHUNK), half] for a in range(chunks)]
        for m in range(modes):
            u_re = pow_ref[0, m, :, half]
            u_im = pow_ref[1, m, :, half]
            for a in range(chunks):
                c_re = coef_re[pl.ds(a * modes + m, 1), :]
                c_im = coef_im[pl.ds(a * modes + m, 1), :]
                totals[a] = totals[a] + (u_re * c_re - u_im * c_im)
        for a in range(chunks):
            at = pl.ds(a * CHUNK, CHUNK)
            stage[at, half] = (query_ref[at, half] * totals[a]).astype(BF16)

    def copy(piece):
        here = pl.ds(pl.multiple_of(piece * span, LANES), span)
        there = pl.ds(pl.multiple_of(base + piece * span, LANES), span)
        return pltpu.make_async_copy(stage.at[:, here], out_ref.at[:, there], sems.at[piece])

    def visit(piece, carry):
        def inner(i, carry):
            tile(aligned(piece * span + i * LANES))
            return carry

        lax.fori_loop(0, span // LANES, inner, 0)
        copy(piece).start()
        return carry

    lax.fori_loop(0, pieces, visit, 0)
    for piece in range(pieces):
        copy(piece).wait()


def is_odd(distance):
    return lax.rem(lax.div(lax.axis_index("seq"), distance), 2) == 1


def pick(flag, a, b):
    return jnp.where(flag, a[0], b[0]), jnp.where(flag, a[1], b[1])


def each_tile(width, body):
    def visit(i, carry):
        body(aligned(i * LANES))
        return carry

    lax.fori_loop(0, width // LANES, visit, 0)


def pair_kernel(mate_ref, total_ref, span_ref, sent_ref, block_ref, early_ref):
    odd = is_odd(1)

    def tile(lanes):
        mate, own = get(mate_ref, lanes), get(total_ref, lanes)
        early, late = pick(odd, mate, own), pick(odd, own, mate)
        block = add(cmul(*get(span_ref, lanes), *early), late)
        put(early_ref, lanes, early)
        put(block_ref, lanes, block)
        put(sent_ref, lanes, block)

    each_tile(total_ref.shape[-1], tile)


def stage_kernel(distance, last, *refs):
    refs = list(refs)
    arrived_ref, span_ref = refs[:2]
    refs = refs[3:]
    block_ref = refs.pop(0)
    enter_ref = refs.pop(0) if distance > 2 else None
    early_ref = refs.pop(0) if last else None
    upper = is_odd(distance)
    odd = is_odd(1)

    def tile(lanes):
        arrived, span = get(arrived_ref, lanes), get(span_ref, lanes)
        moved = arrived
        power = cmul(*span, *span)
        bit = 2
        while bit < distance:
            moved = pick(is_odd(bit), cmul(*power, *moved), moved)
            power = cmul(*power, *power)
            bit *= 2
        enter = jnp.where(upper, moved[0], 0.0), jnp.where(upper, moved[1], 0.0)
        if enter_ref is not None:
            enter = add(enter, get(enter_ref, lanes))
        if last:
            past = add(cmul(*span, *enter), get(early_ref, lanes))
            put(refs[0], lanes, pick(odd, enter, past))
            put(refs[1], lanes, pick(odd, past, enter))
        else:
            block = get(block_ref, lanes)
            block = add(cmul(*power, *pick(upper, arrived, block)), pick(upper, block, arrived))
            put(refs[0], lanes, block)
            put(refs[1], lanes, block)
            put(refs[2], lanes, enter)

    each_tile(span_ref.shape[-1], tile)


def tails_kernel(*refs):
    count = len(refs) - 2
    sources, out_ref, sems = refs[:count], refs[count], refs[count + 1]
    copies = [
        pltpu.make_async_copy(ref.at[pl.ds(ref.shape[0] - ROWS, ROWS), :], out_ref.at[n], sems.at[n])
        for n, ref in enumerate(sources)
    ]
    for copy in copies:
        copy.start()
    for copy in copies:
        copy.wait()


def shards(
    q_proj, k_proj, v_proj, short_taps, pole_rate, pole_angle, residue_re, residue_im, skip_gain
):
    length, channels = q_proj.shape
    branches, short_len = short_taps.shape[:2]
    modes = pole_rate.shape[0]
    half = channels // 2
    chunks = length // CHUNK
    axis_size = lax.axis_size("seq")
    inside = pl.BlockSpec(memory_space=pltpu.VMEM)
    outside = pl.BlockSpec(memory_space=pl.ANY)

    def near(array):
        return pltpu.with_memory_space_constraint(array, pltpu.VMEM)

    def call(kernel, args, outs, scratch, cost, aliases=None, in_specs=None, out_specs=None):
        return pl.pallas_call(
            kernel,
            out_shape=outs,
            in_specs=in_specs or [inside] * len(args),
            out_specs=out_specs or ([inside] * len(outs) if isinstance(outs, list) else inside),
            scratch_shapes=scratch,
            input_output_aliases=aliases or {},
            compiler_params=pltpu.CompilerParams(vmem_limit_bytes=4 << 20),
            cost_estimate=pl.CostEstimate(flops=cost, bytes_accessed=cost, transcendentals=0),
        )(*args)

    def rows(count):
        return pltpu.VMEM((count, LANES), F32)

    def modal(dtype=F32):
        return pltpu.VMEM((2, modes, half), dtype)

    def swap(block, distance):
        return lax.ppermute(block, "seq", [(i, i ^ distance) for i in range(axis_size)])

    gates = pltpu.VMEM((length, half), BF16)
    sums = pltpu.VMEM((chunks, 2, modes, half), F32)
    pads = [rows(length + ROWS), rows(length + ROWS), rows(length), rows(ROWS), rows(ROWS)]

    tails = call(
        tails_kernel, [pltpu.with_memory_space_constraint(x, pltpu.HBM) for x in (q_proj, k_proj, v_proj)], pltpu.VMEM((branches, ROWS, channels), q_proj.dtype),
        [pltpu.SemaphoreType.DMA((branches,))], 1 << 16, in_specs=[outside] * branches,
    )
    rims = lax.ppermute(tails, "seq", [(i, (i + 1) % axis_size) for i in range(axis_size)])
    q, k, v, taps, rate, angle, res_re, res_im, gain = (
        near(array) for array in (
            q_proj, k_proj, v_proj, short_taps, pole_rate, pole_angle, residue_re, residue_im, skip_gain[None]
        )
    )

    gated_o, chunk_o, rest_o, lam_o, step_o, far_o = call(
        functools.partial(states_kernel, False), [k, v, taps, rate, angle],
        [gates, sums, modal(), modal(), modal(), modal()], pads, 16 << 20,
    )
    gated_o, chunk_o, total_o = call(
        head_kernel, [k, v, near(rims), taps, near(lam_o), near(far_o), near(rest_o), near(gated_o), near(chunk_o)],
        [gates, sums, modal(BF16)],
        [rows(CHUNK + ROWS), rows(CHUNK + ROWS), rows(CHUNK), rows(ROWS), rows(ROWS)],
        2 << 20, aliases={7: 0, 8: 1},
    )
    from_mate = swap(total_o, 1)
    gated_m, chunk_m, total_m, lam_m, step_m, span = call(
        functools.partial(states_kernel, True), [k, v, near(rims), taps, rate, angle],
        [gates, sums, modal(), modal(), modal(), modal()], pads, 16 << 20,
    )

    def local(mine, lam, gated, after):
        return call(
            functools.partial(local_kernel, mine),
            [near(after), q, near(rims), taps, gain, res_re, res_im, near(lam), near(gated)],
            [pltpu.VMEM((length, half), F32), pltpu.VMEM((length, half), F32), pltpu.VMEM((2, modes, CHUNK, half), F32)],
            [rows(length + ROWS), rows(2 * length), rows(ROWS), rows(CHUNK * modes), rows(CHUNK * modes),
             rows(6 * modes), rows(8 * modes)],
            8 << 20,
        )

    def finish(mine, enter, chunk, step, made, out=None):
        query, close, power = made
        args = [near(array) for array in (enter, chunk, step, power, query, close)]
        specs = [inside] * len(args)
        aliases = None
        if out is not None:
            args.append(out)
            specs.append(outside)
            aliases = {len(args) - 1: 0}
        pieces = math.gcd(half // LANES, 4)
        return call(
            functools.partial(carried_kernel, mine), args, jax.ShapeDtypeStruct((length, channels), BF16),
            [rows(chunks * modes), rows(chunks * modes), pltpu.VMEM((length, half), BF16),
             pltpu.SemaphoreType.DMA((pieces,))],
            8 << 20, aliases, specs, outside,
        )

    sent, block, early = call(
        pair_kernel, [near(from_mate), near(total_m), near(span)], [modal(BF16), modal(), modal()], [], 1 << 18,
    )
    makers = [functools.partial(local, False, lam_o, gated_o), functools.partial(local, True, lam_m, gated_m)]
    made = []
    enter = []
    distance = 2
    while distance < axis_size:
        last = 2 * distance >= axis_size
        arrived = swap(sent, distance)
        while makers and (last or len(made) * 2 < distance):
            made.append(makers.pop(0)(block))
        args = [arrived, span, made[-1][0], block] + enter + ([early] if last else [])
        results = call(
            functools.partial(stage_kernel, distance, last), [near(array) for array in args],
            [modal(BF16), modal()] if last else [modal(BF16), modal(), modal()], [], 1 << 18,
        )
        if last:
            handed, mine = results
        else:
            sent, block, entered = results
            enter = [entered]
        distance *= 2
    made_o, made_m = made
    handed = swap(handed, 1)
    out = finish(True, mine, chunk_m, step_m, made_m)
    return finish(False, handed, chunk_o, step_o, made_o, out)


def solution(mesh):
    placed = (
        P(("groups", "seq"), "tensor"),
        P(("groups", "seq"), "tensor"),
        P(("groups", "seq"), "tensor"),
        P(None, None, "tensor"),
        P(None, "tensor"),
        P(None, "tensor"),
        P(None, "tensor"),
        P(None, "tensor"),
        P("tensor"),
    )
    return jax.shard_map(
        shards,
        mesh=mesh,
        in_specs=placed,
        out_specs=P(("groups", "seq"), "tensor"),
        check_vma=False,
    )
```
